32 devices in a mesh: seq: 2 (over y), row: 4 (over z), col: 4 (over x, core).
Axes of the slice: x: 2, y: 2, z: 4, core: 2. Of those that a mesh axis runs over, the one named last changes fastest.
Arguments:
- residual_in: float32 [4, 1024, 1152], P('row', 'seq', 'col'), may hold values from -6 to 6
- cotangent: float32 [4, 1024, 1152], P('row', 'seq', 'col'), may hold values from -6 to 6
- heads_weight: float32 [1152, 1536], P('col', 'row'), may hold values from -0.1875 to 0.1875
- output_weight: float32 [1024, 1152], P('row', 'col'), may hold values from -0.1875 to 0.1875
- expand_weight: float32 [2, 1152, 6912], P(None, 'col', 'row'), may hold values from -0.1875 to 0.1875
- shrink_weight: float32 [6912, 1152], P('row', 'col'), may hold values from -0.078125 to 0.078125
- gain_input: float32 [1152], P('col'), may hold values from 0.5 to 1.5
- gain_mixer: float32 [1152], P('col'), may hold values from 0.5 to 1.5
- gain_before: float32 [1152], P('col'), may hold values from 0.5 to 1.5
- gain_after: float32 [1152], P('col'), may hold values from 0.5 to 1.5
- gain_query: float32 [256], replicated, may hold values from 0.5 to 1.5
- gain_key: float32 [256], replicated, may hold values from 0.5 to 1.5
- block_index: int32 [4, 1024], P('col'), may hold values from 0 to 7, never falling along the last dimension, each value on 1 to 256 neighbouring positions
- valid_length: int32 [4], replicated, may hold values from 512 to 1024
- left_heads: float32 [4, 4, 288, 288], P('row', 'col'), may hold values from -1 to 3, as said below
- right_heads: float32 [4, 4, 384, 384], P('row', 'col'), may hold values from -1 to 3, as said below
- leftinv_heads: float32 [4, 4, 288, 288], P('row', 'col'), may hold values from -1 to 3, as said below
- rightinv_heads: float32 [4, 4, 384, 384], P('row', 'col'), may hold values from -1 to 3, as said below
- left_output: float32 [4, 4, 256, 256], P('row', 'col'), may hold values from -1 to 3, as said below
- right_output: float32 [4, 4, 288, 288], P('row', 'col'), may hold values from -1 to 3, as said below
- leftinv_output: float32 [4, 4, 256, 256], P('row', 'col'), may hold values from -1 to 3, as said below
- rightinv_output: float32 [4, 4, 288, 288], P('row', 'col'), may hold values from -1 to 3, as said below
- left_expand: float32 [2, 4, 4, 288, 288], P(None, 'row', 'col'), may hold values from -1 to 3, as said below
- right_expand: float32 [2, 4, 4, 1728, 1728], P(None, 'row', 'col'), may hold values from -1 to 3, as said below
- leftinv_expand: float32 [2, 4, 4, 288, 288], P(None, 'row', 'col'), may hold values from -1 to 3, as said below
- rightinv_expand: float32 [2, 4, 4, 1728, 1728], P(None, 'row', 'col'), may hold values from -1 to 3, as said below
- left_shrink: float32 [4, 4, 1728, 1728], P('row', 'col'), may hold values from -1 to 3, as said below
- right_shrink: float32 [4, 4, 288, 288], P('row', 'col'), may hold values from -1 to 3, as said below
- leftinv_shrink: float32 [4, 4, 1728, 1728], P('row', 'col'), may hold values from -1 to 3, as said below
- rightinv_shrink: float32 [4, 4, 288, 288], P('row', 'col'), may hold values from -1 to 3, as said below
Outputs:
- block_out: float32 [4, 1024, 1152], P('row', 'seq', 'col')
- input_slope: float32 [4, 1024, 1152], P('row', 'seq', 'col')
- slope_input: float32 [1152], P('col')
- slope_mixer: float32 [1152], P('col')
- slope_before: float32 [1152], P('col')
- slope_after: float32 [1152], P('col')
- slope_query: float32 [256], replicated
- slope_key: float32 [256], replicated
- slope_heads: float32 [1152, 1536], P('col', 'row')
- master_heads: float32 [1152, 1536], P('col', 'row')
- newleft_heads: float32 [4, 4, 288, 288], P('row', 'col')
- newright_heads: float32 [4, 4, 384, 384], P('row', 'col')
- slope_output: float32 [1024, 1152], P('row', 'col')
- master_output: float32 [1024, 1152], P('row', 'col')
- newleft_output: float32 [4, 4, 256, 256], P('row', 'col')
- newright_output: float32 [4, 4, 288, 288], P('row', 'col')
- slope_expand: float32 [2, 1152, 6912], P(None, 'col', 'row')
- master_expand: float32 [2, 1152, 6912], P(None, 'col', 'row')
- newleft_expand: float32 [2, 4, 4, 288, 288], P(None, 'row', 'col')
- newright_expand: float32 [2, 4, 4, 1728, 1728], P(None, 'row', 'col')
- slope_shrink: float32 [6912, 1152], P('row', 'col')
- master_shrink: float32 [6912, 1152], P('row', 'col')
- newleft_shrink: float32 [4, 4, 1728, 1728], P('row', 'col')
- newright_shrink: float32 [4, 4, 288, 288], P('row', 'col')
- level_stream: float32 [], replicated
- level_mixer: float32 [], replicated
- level_feed: float32 [], replicated
The draws below stay inside these ranges and needn't reach their ends.
Inputs may be any that keep to these rules, and one draw needn't show every extreme that they name: `block_index`: within a sequence the block numbers never fall, each block holds 1 to 256 positions. `left_heads`: each block a symmetric positive definite matrix. `right_heads`: each block a symmetric positive definite matrix. `leftinv_heads`: each block a symmetric positive definite matrix. `rightinv_heads`: each block a symmetric positive definite matrix. `left_output`: each block a symmetric positive definite matrix. `right_output`: each block a symmetric positive definite matrix. `leftinv_output`: each block a symmetric positive definite matrix. `rightinv_output`: each block a symmetric positive definite matrix. `left_expand`: each block a symmetric positive definite matrix. `right_expand`: each block a symmetric positive definite matrix. `leftinv_expand`: each block a symmetric positive definite matrix. `rightinv_expand`: each block a symmetric positive definite matrix. `left_shrink`: each block a symmetric positive definite matrix. `right_shrink`: each block a symmetric positive definite matrix. `leftinv_shrink`: each block a symmetric positive definite matrix. `rightinv_shrink`: each block a symmetric positive definite matrix.
All inputs are finite; a program needn't handle non-finite values.
Results may differ from the reference program's by a relative error of at most 0.018.
Values may be sent and summed in bfloat16 or wider, within the bound.
No kernel may reach another device: no remote copies, remote signals or barrier semaphores. Data moves between devices by JAX's collectives and lax.ppermute only.
A program may use at most 320 MiB of HBM per device.

```python
import math
import jax
import jax.numpy as jnp
import numpy as np
from jax import lax

D = 1152
HEADS = 4
HD = 256
FF = 6912
BLK = 256
QW = 1024
QKV = 1536
LEN = 1024
SEQS = 4
TOKENS = 4096
NBLK = 8
GR = 4
GC = 4
DC = 288
QKVR = 384
HR = 256
FR = 1728


def spread_matrix(key, lead, size):
    first, second = jax.random.split(key)
    noise = jax.random.normal(first, lead + (size, size), jnp.float32)
    noise = (noise + jnp.swapaxes(noise, -1, -2)) * (0.2 / (2.0 * size) ** 0.5)
    noise = jnp.clip(noise, -0.5, 0.5)
    diagonal = jax.random.uniform(second, lead + (size,), jnp.float32, 0.5, 1.5)
    eye = jnp.eye(size, dtype=jnp.float32)
    return noise * (1.0 - eye) + eye * diagonal[..., None, :]


def draw_left_heads(key, part):
    return spread_matrix(jax.random.fold_in(key, 1), (GR, GC), DC)


def draw_right_heads(key, part):
    return spread_matrix(jax.random.fold_in(key, 2), (GR, GC), QKVR)


def draw_leftinv_heads(key, part):
    return spread_matrix(jax.random.fold_in(key, 3), (GR, GC), DC)


def draw_rightinv_heads(key, part):
    return spread_matrix(jax.random.fold_in(key, 4), (GR, GC), QKVR)


def draw_left_output(key, part):
    return spread_matrix(jax.random.fold_in(key, 5), (GR, GC), HR)


def draw_right_output(key, part):
    return spread_matrix(jax.random.fold_in(key, 6), (GR, GC), DC)


def draw_leftinv_output(key, part):
    return spread_matrix(jax.random.fold_in(key, 7), (GR, GC), HR)


def draw_rightinv_output(key, part):
    return spread_matrix(jax.random.fold_in(key, 8), (GR, GC), DC)


def draw_left_expand(key, part):
    return spread_matrix(jax.random.fold_in(key, 9), (2, GR, GC), DC)


def draw_right_expand(key, part):
    return spread_matrix(jax.random.fold_in(key, 10), (2, GR, GC), FR)


def draw_leftinv_expand(key, part):
    return spread_matrix(jax.random.fold_in(key, 11), (2, GR, GC), DC)


def draw_rightinv_expand(key, part):
    return spread_matrix(jax.random.fold_in(key, 12), (2, GR, GC), FR)


def draw_left_shrink(key, part):
    return spread_matrix(jax.random.fold_in(key, 13), (GR, GC), FR)


def draw_right_shrink(key, part):
    return spread_matrix(jax.random.fold_in(key, 14), (GR, GC), DC)


def draw_leftinv_shrink(key, part):
    return spread_matrix(jax.random.fold_in(key, 15), (GR, GC), FR)


def draw_rightinv_shrink(key, part):
    return spread_matrix(jax.random.fold_in(key, 16), (GR, GC), DC)


def with_ends(array, rng, low, largest):
    dims = array.shape
    place = [jax.random.randint(jax.random.fold_in(rng, axis), (), 0, dims[axis]) for axis in range(len(dims))]
    array = array.at[tuple(place)].set(low)
    longest = dims.index(max(dims))
    place[longest] = (place[longest] + 1) % dims[longest]
    return array.at[tuple(place)].set(largest)


def block_scale(own_key, shape, pieces, least, top_value):
    factor_of, own = 1.0, jax.random.fold_in(own_key, 6)
    for axis_at, blocks in pieces:
        draws = jnp.exp(jax.random.uniform(jax.random.fold_in(own, axis_at), (blocks,), jnp.float32, least / len(pieces), top_value / len(pieces)))
        factor_of = factor_of * jnp.repeat(draws, shape[axis_at] // blocks).reshape([-1 if axis == axis_at else 1 for axis in range(len(shape))])
    return factor_of


def profile(amount, total, bound, lean):
    loads = [(1 << 20) // math.isqrt(standing ** lean) + 1 for standing in range(2, amount + 1)]
    rest, holding = total - bound - (amount - 1), [1] * (amount - 1)
    while rest > 0:
        candidates = [i for i in range(amount - 1) if holding[i] < bound]
        mass, remaining = sum([loads[i] for i in candidates]), rest
        for i in candidates:
            more = min(bound - holding[i], max(1, remaining * loads[i] // mass), rest)
            holding[i] = holding[i] + more
            rest = rest - more
    return np.array([bound] + holding)


def uneven(rng, count, total, bound, skew):
    if count == 2:
        one = jax.random.randint(rng, (), max(1, total - bound), min(bound, total - 1) + 1)
        return jnp.stack([one, total - one])
    tallies = jnp.asarray(profile(count, total, bound, skew), jnp.int32)
    twos = (count - 1) // 2
    source_of, taker = tallies[1:1 + 2 * twos:2], tallies[2:2 + 2 * twos:2]
    room = jnp.minimum(source_of - 1, bound - taker)
    moved = jax.random.randint(jax.random.fold_in(rng, 1), (twos,), 0, 1 << 20) % (room + 1)
    tallies = tallies.at[1:1 + 2 * twos:2].set(source_of - moved).at[2:2 + 2 * twos:2].set(taker + moved)
    return tallies[jax.random.permutation(jax.random.fold_in(rng, 2), count)]


def centred(key, dims, spread, bound, cuts=(), held_as=jnp.bfloat16):
    entries = jax.random.normal(key, dims, jnp.float32) * spread
    if len(cuts) > 0:
        entries = block_scale(key, dims, cuts, -0.22, 0.18) * entries
    return jnp.clip(entries, min=-bound, max=bound).astype(held_as)


def setup_inputs(seed: int = 0) -> dict:
    key_list = jax.random.split(jax.random.key(seed), 31)
    residual_in = centred(key_list[0], (SEQS, LEN, D), 1.0, 6.0, ((0, 4), (1, 2), (2, 4)), jnp.float32)
    cotangent = centred(key_list[1], (SEQS, LEN, D), 1.0, 6.0, ((0, 4), (1, 2), (2, 4)), jnp.float32)
    heads_weight = centred(key_list[2], (D, QKV), D ** -0.5, 0.1875, ((0, 4), (1, 4)), jnp.float32)
    output_weight = centred(key_list[3], (QW, D), QW ** -0.5, 0.1875, ((0, 4), (1, 4)), jnp.float32)
    expand_weight = centred(key_list[4], (2, D, FF), D ** -0.5, 0.1875, ((1, 4), (2, 4)), jnp.float32)
    shrink_weight = centred(key_list[5], (FF, D), FF ** -0.5, 0.078125, ((0, 4), (1, 4)), jnp.float32)
    gain_input = jnp.clip(1.0 + 0.1 * jax.random.normal(key_list[6], (D,), jnp.float32), 0.5, 1.5)
    gain_mixer = jnp.clip(1.0 + 0.1 * jax.random.normal(key_list[7], (D,), jnp.float32), 0.5, 1.5)
    gain_before = jnp.clip(1.0 + 0.1 * jax.random.normal(key_list[8], (D,), jnp.float32), 0.5, 1.5)
    gain_after = jnp.clip(1.0 + 0.1 * jax.random.normal(key_list[9], (D,), jnp.float32), 0.5, 1.5)
    gain_query = jnp.clip(1.0 + 0.1 * jax.random.normal(key_list[10], (HD,), jnp.float32), 0.5, 1.5)
    gain_key = jnp.clip(1.0 + 0.1 * jax.random.normal(key_list[11], (HD,), jnp.float32), 0.5, 1.5)
    block_index = jax.vmap(lambda own: jnp.searchsorted(jnp.cumsum(uneven(own, NBLK, LEN, BLK, 0)), jnp.arange(LEN), side="right"))(jax.random.split(key_list[12], SEQS)).reshape((SEQS, LEN)).astype(jnp.int32)
    valid_length = with_ends(jax.random.randint(key_list[13], (SEQS,), LEN // 2, LEN + 1), jax.random.fold_in(key_list[13], 1), LEN // 2, LEN).astype(jnp.int32)
    left_heads = draw_left_heads(jax.random.fold_in(key_list[30], 71), 0)
    right_heads = draw_right_heads(jax.random.fold_in(key_list[30], 71), 0)
    leftinv_heads = draw_leftinv_heads(jax.random.fold_in(key_list[30], 71), 0)
    rightinv_heads = draw_rightinv_heads(jax.random.fold_in(key_list[30], 71), 0)
    left_output = draw_left_output(jax.random.fold_in(key_list[30], 71), 0)
    right_output = draw_right_output(jax.random.fold_in(key_list[30], 71), 0)
    leftinv_output = draw_leftinv_output(jax.random.fold_in(key_list[30], 71), 0)
    rightinv_output = draw_rightinv_output(jax.random.fold_in(key_list[30], 71), 0)
    left_expand = draw_left_expand(jax.random.fold_in(key_list[30], 71), 0)
    right_expand = draw_right_expand(jax.random.fold_in(key_list[30], 71), 0)
    leftinv_expand = draw_leftinv_expand(jax.random.fold_in(key_list[30], 71), 0)
    rightinv_expand = draw_rightinv_expand(jax.random.fold_in(key_list[30], 71), 0)
    left_shrink = draw_left_shrink(jax.random.fold_in(key_list[30], 71), 0)
    right_shrink = draw_right_shrink(jax.random.fold_in(key_list[30], 71), 0)
    leftinv_shrink = draw_leftinv_shrink(jax.random.fold_in(key_list[30], 71), 0)
    rightinv_shrink = draw_rightinv_shrink(jax.random.fold_in(key_list[30], 71), 0)
    return {"residual_in": residual_in, "cotangent": cotangent, "heads_weight": heads_weight, "output_weight": output_weight, "expand_weight": expand_weight, "shrink_weight": shrink_weight, "gain_input": gain_input, "gain_mixer": gain_mixer, "gain_before": gain_before, "gain_after": gain_after, "gain_query": gain_query, "gain_key": gain_key, "block_index": block_index, "valid_length": valid_length, "left_heads": left_heads, "right_heads": right_heads, "leftinv_heads": leftinv_heads, "rightinv_heads": rightinv_heads, "left_output": left_output, "right_output": right_output, "leftinv_output": leftinv_output, "rightinv_output": rightinv_output, "left_expand": left_expand, "right_expand": right_expand, "leftinv_expand": leftinv_expand, "rightinv_expand": rightinv_expand, "left_shrink": left_shrink, "right_shrink": right_shrink, "leftinv_shrink": leftinv_shrink, "rightinv_shrink": rightinv_shrink}


@jax.custom_vjp
def lower_factor(v):
    return lax.optimization_barrier(v.astype(jnp.bfloat16)).astype(jnp.float32)

@jax.custom_vjp
def lower_factor_back(v):
    return v

def low_keep(v):
    return (lower_factor(v), None)

def low_pass(kept, grad):
    return (grad,)

def back_keep(v):
    return (v, None)

def back_low(kept, grad):
    return (lower_factor(grad),)
lower_factor.defvjp(low_keep, low_pass)
lower_factor_back.defvjp(back_keep, back_low)
eps_norm = 1e-06
theta = 1000000.0
score_scale = 0.0625
rate = 0.05
decay = 0.5
highest = lax.Precision.HIGHEST

def matrix_product(form, first, second):
    return jnp.einsum(form, first, second, precision=highest)

def norm(values, gain):
    return values * lax.rsqrt(lax.optimization_barrier(jnp.mean(values * values, axis=-1, keepdims=True)) + eps_norm) * gain

def rotate(values, cosine, sine):
    half = values.shape[-1] // 2
    first = values[..., :half]
    second = values[..., half:]
    return jnp.concatenate([first * cosine - second * sine, second * cosine + first * sine], axis=-1)

def attention(query_r, key_r, value, block_index, keep_key):
    width = min(512, LEN)
    count = LEN // width
    query_parts = jnp.moveaxis(query_r.reshape(SEQS, count, width, HEADS, HD), 1, 0)
    block_parts = jnp.moveaxis(block_index.reshape(SEQS, count, width), 1, 0)

    def one_part(pair):
        query_part, block_part = pair
        scores = lower_factor_back(matrix_product('sqhd,skd->sqhk', query_part, key_r) * score_scale)
        allowed = (block_index[:, None, :] <= block_part[:, :, None]) & keep_key[:, None, :]
        scores = jnp.where(allowed[:, :, None, :], scores, -1e+30)
        top = lax.optimization_barrier(jnp.max(scores, axis=-1, keepdims=True))
        weight = jnp.exp(scores - top)
        prob = weight / lax.optimization_barrier(jnp.sum(weight, axis=-1, keepdims=True))
        return matrix_product('sqhk,skd->sqhd', lower_factor(prob), value)
    parts = lax.map(jax.checkpoint(one_part), (query_parts, block_parts))
    return jnp.moveaxis(parts, 0, 1).reshape(SEQS, LEN, QW)

def shampoo(slope, weight, left, right, left_inv, right_inv):
    rows = slope.shape[-2]
    cols = slope.shape[-1]
    turned = jnp.swapaxes(slope, -1, -2)
    new_left = decay * left + (1.0 - decay) * jnp.matmul(slope, turned, precision=highest) / cols
    new_right = decay * right + (1.0 - decay) * jnp.matmul(turned, slope, precision=highest) / rows
    step = jnp.matmul(jnp.matmul(left_inv, slope, precision=highest), right_inv, precision=highest)
    return (weight - rate * step, new_left, new_right)

def heads_blocks(matrix):
    return jnp.transpose(matrix.reshape(GC, DC, GR, QKVR), (2, 0, 1, 3))

def heads_layout(blocks):
    return jnp.transpose(blocks, (1, 2, 0, 3)).reshape(D, QKV)

def rows_blocks(matrix, piece):
    return jnp.transpose(matrix.reshape(GR, piece, GC, DC), (0, 2, 1, 3))

def rows_layout(blocks, piece):
    return jnp.transpose(blocks, (0, 2, 1, 3)).reshape(GR * piece, D)

def expand_blocks(tensor):
    return jnp.transpose(tensor.reshape(2, GC, DC, GR, FR), (0, 3, 1, 2, 4))

def expand_layout(blocks):
    return jnp.transpose(blocks, (0, 2, 3, 1, 4)).reshape(2, D, FF)

def reference(residual_in, cotangent, heads_weight, output_weight, expand_weight, shrink_weight, gain_input, gain_mixer, gain_before, gain_after, gain_query, gain_key, block_index, valid_length, left_heads, right_heads, leftinv_heads, rightinv_heads, left_output, right_output, leftinv_output, rightinv_output, left_expand, right_expand, leftinv_expand, rightinv_expand, left_shrink, right_shrink, leftinv_shrink, rightinv_shrink):
    single_float32 = jnp.float32
    positions = jnp.arange(LEN).astype(jnp.int32)
    half = HD // 2
    freq = theta ** (-(jnp.arange(half).astype(single_float32) * 2.0) / HD)
    angle = positions.astype(single_float32)[:, None] * freq[None, :]
    cosine = jnp.cos(angle)
    sine = jnp.sin(angle)
    keep_key = positions[None, :] < valid_length[:, None]

    def layer(stream_in, heads_matrix, output_matrix, expand_matrix, shrink_matrix, g_input, g_mixer, g_before, g_after, g_query, g_key):
        input_activation = lower_factor(norm(stream_in, g_input))
        query_key_value = lower_factor_back(lower_factor(matrix_product('rhi,io->rho', input_activation, lower_factor(heads_matrix))))
        query = query_key_value[..., :QW].reshape(SEQS, LEN, HEADS, HD)
        keyed = query_key_value[..., QW:QW + HD]
        valued = query_key_value[..., QW + HD:]
        query_r = lower_factor(rotate(norm(query, g_query), cosine[:, None, :], sine[:, None, :]))
        key_r = lower_factor(rotate(norm(keyed, g_key), cosine, sine))
        attended_values = lower_factor_back(lower_factor(attention(query_r, key_r, valued, block_index, keep_key)))
        attention_output = lower_factor_back(matrix_product('rji,ix->rjx', attended_values, lower_factor(output_matrix)))
        branch_one = norm(attention_output, g_mixer)
        stream = stream_in + branch_one
        feed_activation = lower_factor(norm(stream, g_before))
        gate_values = lower_factor_back(matrix_product('rhi,io->rho', feed_activation, lower_factor(expand_matrix[0])))
        upper_factor = lower_factor_back(matrix_product('rhi,io->rho', feed_activation, lower_factor(expand_matrix[1])))
        hidden_state = lower_factor(jax.nn.gelu(gate_values, approximate=True) * upper_factor)
        feed_output = lower_factor_back(matrix_product('rji,ix->rjx', hidden_state, lower_factor(shrink_matrix)))
        branch_two = norm(feed_output, g_after)
        return (stream + branch_two, branch_one, branch_two)
    primals = (residual_in.astype(single_float32), heads_weight.astype(single_float32), output_weight.astype(single_float32), expand_weight.astype(single_float32), shrink_weight.astype(single_float32), gain_input.astype(single_float32), gain_mixer.astype(single_float32), gain_before.astype(single_float32), gain_after.astype(single_float32), gain_query.astype(single_float32), gain_key.astype(single_float32))
    outs, pullback = jax.vjp(layer, *primals)
    block_out, branch_one, branch_two = outs
    grads = pullback((cotangent.astype(single_float32), jnp.zeros_like(branch_one), jnp.zeros_like(branch_two)))
    inverse_root = 1.0 / math.sqrt(TOKENS)
    input_slope = grads[0]
    g_heads = heads_blocks(grads[1] * inverse_root)
    g_output = rows_blocks(grads[2] * inverse_root, HR)
    g_expand = expand_blocks(grads[3] * inverse_root)
    g_shrink = rows_blocks(grads[4] * inverse_root, FR)
    m_heads, nl_heads, nr_heads = shampoo(g_heads, heads_blocks(heads_weight), left_heads, right_heads, leftinv_heads, rightinv_heads)
    m_output, nl_output, nr_output = shampoo(g_output, rows_blocks(output_weight, HR), left_output, right_output, leftinv_output, rightinv_output)
    m_expand, nl_expand, nr_expand = shampoo(g_expand, expand_blocks(expand_weight), left_expand, right_expand, leftinv_expand, rightinv_expand)
    m_shrink, nl_shrink, nr_shrink = shampoo(g_shrink, rows_blocks(shrink_weight, FR), left_shrink, right_shrink, leftinv_shrink, rightinv_shrink)
    valid = keep_key.astype(single_float32)[..., None]
    count = jnp.sum(valid_length).astype(single_float32) * D
    level_stream = jnp.sqrt(jnp.sum(block_out * block_out * valid) / count)
    level_mixer = jnp.sqrt(jnp.sum(branch_one * branch_one * valid) / count)
    level_feed = jnp.sqrt(jnp.sum(branch_two * branch_two * valid) / count)
    return (block_out, input_slope, grads[5] * inverse_root, grads[6] * inverse_root, grads[7] * inverse_root, grads[8] * inverse_root, grads[9] * inverse_root, grads[10] * inverse_root, heads_layout(g_heads), heads_layout(m_heads), nl_heads, nr_heads, rows_layout(g_output, HR), rows_layout(m_output, HR), nl_output, nr_output, expand_layout(g_expand), expand_layout(m_expand), nl_expand, nr_expand, rows_layout(g_shrink, FR), rows_layout(m_shrink, FR), nl_shrink, nr_shrink, level_stream, level_mixer, level_feed)
```

```python
import math

import jax
import jax.numpy as jnp
from jax import lax
from jax.sharding import PartitionSpec as P

D = 1152
HEADS = 4
HD = 256
QW = 1024

eps_norm = 1e-06
theta = 1000000.0
score_scale = 0.0625
rate = 0.05
decay = 0.5
f32 = jnp.float32
b16 = jnp.bfloat16


ORDER = (0, 2, 1, 3)


def swap(values, axis, step):
    return lax.ppermute(values, axis, [(i, i ^ step) for i in range(lax.axis_size(axis))])


def bits_of(axis):
    return [1 << b for b in range(lax.axis_size(axis).bit_length() - 1)]


def col_gather(values):
    near = jnp.stack([values, swap(values, "col", 2)])
    return jnp.concatenate([near, swap(near, "col", 1)])


def col_reduce(parts):
    near = parts[:2].astype(f32) + swap(parts[2:], "col", 1).astype(f32)
    return near[0] + swap(near[1].astype(b16), "col", 2).astype(f32)


def row_gather(values):
    return jnp.stack([values] + [swap(values, "row", j) for j in range(1, lax.axis_size("row"))])


def row_reduce(parts):
    total = parts[0]
    for j in range(1, lax.axis_size("row")):
        total = total + swap(parts[j].astype(b16), "row", j).astype(f32)
    return total


def seq_sum(values):
    for step in bits_of("seq"):
        sent = values.astype(b16)
        values = lax.reduce_precision(values, 8, 7) + swap(sent, "seq", step).astype(f32)
    return values


def plane_gather(values):
    stack = values[None]
    stack = jnp.concatenate([stack, swap(stack, "col", 2)])
    for step in bits_of("seq"):
        stack = jnp.concatenate([stack, swap(stack, "seq", step)])
    return jnp.concatenate([stack, swap(stack, "col", 1)])


def plane_reduce(parts):
    def halve(parts, axis, step):
        half = parts.shape[0] // 2
        return parts[:half] + swap(parts[half:].astype(b16), axis, step).astype(f32)

    parts = halve(parts, "col", 1)
    for step in reversed(bits_of("seq")):
        parts = halve(parts, "seq", step)
    return halve(parts, "col", 2)[0]


def plane_blocks():
    seqs = lax.axis_size("seq")
    s, c = lax.axis_index("seq"), lax.axis_index("col")
    out = []
    for core in range(2):
        for j in range(seqs):
            for x in range(2):
                out.append((s ^ j, c ^ (2 * x + core)))
    return out


def to_tokens(values):
    c = lax.axis_index("col")
    sub = values.shape[0] // 4
    pieces = []
    for j in ORDER:
        piece = lax.dynamic_slice_in_dim(values, (c ^ j) * sub, sub)
        pieces.append(swap(piece, "col", j) if j else piece)
    return jnp.concatenate(pieces, axis=1)


def to_features(values):
    c = lax.axis_index("col")
    wide = values.shape[1] // 4
    pieces = []
    for n, j in enumerate(ORDER):
        piece = values[:, n * wide : (n + 1) * wide]
        pieces.append(swap(piece, "col", j) if j else piece)
    stack = jnp.stack([pieces[ORDER.index(j)] for j in range(4)])
    return jnp.concatenate(
        [lax.dynamic_index_in_dim(stack, c ^ a, 0, keepdims=False) for a in range(4)]
    )


def row_absolute(stack):
    r = lax.axis_index("row")
    return jnp.concatenate(
        [
            lax.dynamic_index_in_dim(stack, r ^ a, 0, keepdims=False)
            for a in range(stack.shape[0])
        ],
        axis=1,
    )


def row_relative(values):
    r = lax.axis_index("row")
    rows = lax.axis_size("row")
    wide = values.shape[1] // rows
    return jnp.concatenate(
        [lax.dynamic_slice_in_dim(values, (r ^ j) * wide, wide, axis=1) for j in range(rows)],
        axis=1,
    )


def mm(first, second):
    return lax.dot_general(first, second, (((1,), (0,)), ((), ())), preferred_element_type=f32)


def mm_nt(first, second):
    return lax.dot_general(first, second, (((1,), (1,)), ((), ())), preferred_element_type=f32)


def mm_tn(first, second):
    return lax.dot_general(first, second, (((0,), (0,)), ((), ())), preferred_element_type=f32)


def inverse_norm(values):
    return lax.rsqrt(jnp.mean(values * values, axis=-1, keepdims=True) + eps_norm)


def norm_back(values, inverse, gain, upstream):
    scaled = upstream * gain
    inner = jnp.mean(values * scaled, axis=-1, keepdims=True)
    lower = inverse * scaled - values * (inverse * inverse * inverse * inner)
    return lower, upstream * values * inverse


def rotate(values, cosine, sine):
    half = values.shape[-1] // 2
    first, second = values[..., :half], values[..., half:]
    return jnp.concatenate(
        [first * cosine - second * sine, second * cosine + first * sine], axis=-1
    )


def rotate_back(upstream, cosine, sine):
    half = upstream.shape[-1] // 2
    first, second = upstream[..., :half], upstream[..., half:]
    return jnp.concatenate(
        [first * cosine + second * sine, second * cosine - first * sine], axis=-1
    )


def shampoo(total, scale, weight, left, right, left_inv, right_inv):
    m, n = total.shape
    low = total.astype(b16)
    new_left = decay * left + ((1.0 - decay) * scale * scale / n) * mm_nt(low, low)
    new_right = decay * right + ((1.0 - decay) * scale * scale / m) * mm_tn(low, low)
    step = mm(mm(left_inv.astype(b16), low).astype(b16), right_inv.astype(b16))
    return weight - (rate * scale) * step, new_left, new_right


def per_device(
    residual_in,
    cotangent,
    heads_weight,
    output_weight,
    expand_weight,
    shrink_weight,
    gain_input,
    gain_mixer,
    gain_before,
    gain_after,
    gain_query,
    gain_key,
    block_index,
    valid_length,
    left_heads,
    right_heads,
    leftinv_heads,
    rightinv_heads,
    left_output,
    right_output,
    leftinv_output,
    rightinv_output,
    left_expand,
    right_expand,
    leftinv_expand,
    rightinv_expand,
    left_shrink,
    right_shrink,
    leftinv_shrink,
    rightinv_shrink,
):
    _, group, dc = residual_in.shape
    all_seqs = valid_length.shape[0]
    col_seqs, length = block_index.shape
    rows, seqs = lax.axis_size("row"), lax.axis_size("seq")
    r, s, c = lax.axis_index("row"), lax.axis_index("seq"), lax.axis_index("col")
    sub = group // 4
    wide = expand_weight.shape[2]
    inverse_root = 1.0 / math.sqrt(all_seqs * length)

    x = to_tokens(residual_in[0])
    gains = col_gather(jnp.stack([gain_input, gain_mixer, gain_before, gain_after]))
    gains = jnp.transpose(gains, (1, 0, 2)).reshape(4, 1, D)
    g_input, g_mixer, g_before, g_after = gains[0], gains[1], gains[2], gains[3]
    heads_full = col_gather(row_absolute(row_gather(heads_weight.astype(b16)))).reshape(D, -1)
    output_full = col_gather(
        row_absolute(row_gather(jnp.transpose(output_weight).astype(b16)))
    ).reshape(D, QW)
    gate_full = col_gather(expand_weight[0].astype(b16)).reshape(D, wide)
    upper_full = col_gather(expand_weight[1].astype(b16)).reshape(D, wide)
    shrink_full = col_gather(jnp.transpose(shrink_weight).astype(b16)).reshape(D, wide)
    cot = to_tokens(cotangent[0])

    own_length = lax.dynamic_index_in_dim(valid_length, r, 0, keepdims=False)
    start = s * group + c * sub
    positions = start + jnp.arange(sub)
    valid = (positions < own_length).astype(f32)[:, None]
    held = jnp.stack([block_index] + [swap(block_index, "col", j) for j in (1, 2, 3)])
    held = lax.dynamic_index_in_dim(held, c ^ (r // col_seqs), 0, keepdims=False)
    blocks = lax.dynamic_index_in_dim(held, r % col_seqs, 0, keepdims=False)
    plane = plane_blocks()
    key_starts = jnp.stack([a * group + b * sub for a, b in plane])
    key_positions = (key_starts[:, None] + jnp.arange(sub)[None, :]).reshape(-1)
    key_blocks = jnp.take(
        blocks.reshape(4 * seqs, sub), jnp.stack([a * 4 + b for a, b in plane]), axis=0
    ).reshape(-1)
    query_blocks = lax.dynamic_slice_in_dim(blocks, start, sub)
    allowed = (key_blocks[None, :] <= query_blocks[:, None]) & (key_positions < own_length)[None, :]
    half = HD // 2
    freq = theta ** (-(jnp.arange(half).astype(f32) * 2.0) / HD)
    angle = positions.astype(f32)[:, None] * freq[None, :]
    cosine, sine = jnp.cos(angle), jnp.sin(angle)

    inv_in = inverse_norm(x)
    act_in = (x * inv_in * g_input).astype(b16)
    qkv = mm(act_in, heads_full).astype(b16)
    query = jnp.stack([qkv[:, h * HD : (h + 1) * HD] for h in range(HEADS)]).astype(f32)
    keyed = qkv[:, QW : QW + HD].astype(f32)
    key_inv = inverse_norm(keyed)
    key_r = rotate(keyed * key_inv * gain_key, cosine, sine).astype(b16)
    keys_values = plane_gather(jnp.concatenate([key_r, qkv[:, QW + HD :]], axis=1))
    keys_values = keys_values.reshape(-1, 2 * HD)
    keys_all, values_all = keys_values[:, :HD], keys_values[:, HD:]
    query_inv = inverse_norm(query)
    query_r = rotate(query * query_inv * gain_query, cosine, sine).astype(b16)
    query_r = query_r.reshape(HEADS * sub, HD)
    scores = (mm_nt(query_r, keys_all) * score_scale).reshape(HEADS, sub, -1)
    scores = jnp.where(allowed[None], scores, -1e30)
    top = jnp.max(scores, axis=-1, keepdims=True)
    weight = jnp.exp(scores - top)
    prob = (weight / jnp.sum(weight, axis=-1, keepdims=True)).reshape(HEADS * sub, -1)
    prob_b = prob.astype(b16)
    attended = mm(prob_b, values_all).astype(b16).reshape(HEADS, sub, HD)
    attended = jnp.concatenate([attended[h] for h in range(HEADS)], axis=1)
    attn_out = mm_nt(attended, output_full)
    inv_mix = inverse_norm(attn_out)
    branch_one = attn_out * inv_mix * g_mixer
    stream = x + branch_one
    inv_before = inverse_norm(stream)
    act_ff = (stream * inv_before * g_before).astype(b16)

    act_full = row_gather(act_ff).reshape(rows * sub, D)
    gate = mm(act_full, gate_full)
    upper = mm(act_full, upper_full)
    root = math.sqrt(2.0 / math.pi)
    tanh = jnp.tanh(root * (gate + 0.044715 * gate * gate * gate))
    gelu = 0.5 * gate * (1.0 + tanh)
    hidden = (gelu * upper).astype(b16)
    ff_out = row_reduce(mm_nt(hidden, shrink_full).reshape(rows, sub, D))
    inv_after = inverse_norm(ff_out)
    branch_two = ff_out * inv_after * g_after
    block_out = stream + branch_two

    d_ff, after_part = norm_back(ff_out, inv_after, g_after, cot)
    d_ff_full = row_gather(d_ff.astype(b16)).reshape(rows * sub, D)
    d_hidden = mm(d_ff_full, shrink_full)
    slope = 0.5 * (1.0 + tanh) + 0.5 * gate * (1.0 - tanh * tanh) * (
        root * (1.0 + 3.0 * 0.044715 * gate * gate)
    )
    d_gate = (d_hidden * upper * slope).astype(b16)
    d_upper = (d_hidden * gelu).astype(b16)
    d_act = mm_nt(d_gate, gate_full) + mm_nt(d_upper, upper_full)
    d_act_ff = row_reduce(d_act.reshape(rows, sub, D))
    shrink_sum = seq_sum(col_reduce(mm_tn(d_ff_full, hidden).astype(b16).reshape(4, dc, wide)))
    gate_sum = seq_sum(col_reduce(mm_tn(act_full, d_gate).astype(b16).reshape(4, dc, wide)))
    upper_sum = seq_sum(col_reduce(mm_tn(act_full, d_upper).astype(b16).reshape(4, dc, wide)))

    d_stream_norm, before_part = norm_back(stream, inv_before, g_before, d_act_ff)
    d_stream = cot + d_stream_norm
    d_attn, mixer_part = norm_back(attn_out, inv_mix, g_mixer, d_stream)
    d_attn = d_attn.astype(b16)
    d_mixer = mm(d_attn, output_full).astype(b16)
    d_attended = jnp.concatenate(
        [d_mixer[:, h * HD : (h + 1) * HD] for h in range(HEADS)]
    )
    d_prob = mm_nt(d_attended, values_all)
    delta = jnp.sum(prob * d_prob, axis=-1, keepdims=True)
    d_score = (prob * (d_prob - delta)).astype(b16)
    d_key_part = mm_tn(d_score, query_r) * score_scale
    d_value_part = mm_tn(prob_b, d_attended)
    d_kv = jnp.concatenate([d_key_part, d_value_part], axis=1)
    d_kv = plane_reduce(d_kv.reshape(-1, sub, 2 * HD))
    d_query_r = (mm(d_score, keys_all) * score_scale).reshape(HEADS, sub, HD)
    d_query, query_part = norm_back(
        query, query_inv, gain_query, rotate_back(d_query_r, cosine, sine)
    )
    d_key, key_part = norm_back(
        keyed, key_inv, gain_key, rotate_back(d_kv[:, :HD], cosine, sine)
    )
    d_qkv = jnp.concatenate([d_query[h] for h in range(HEADS)] + [d_key, d_kv[:, HD:]], axis=1)
    d_qkv = d_qkv.astype(b16)
    d_act_in = mm_nt(d_qkv, heads_full)
    d_input_norm, input_part = norm_back(x, inv_in, g_input, d_act_in)
    input_slope = d_stream + d_input_norm

    def spread_sum(first, second):
        blocks_sum = mm_tn(first, row_relative(second)).astype(b16).reshape(4, dc, -1)
        near = col_reduce(blocks_sum)
        near = jnp.stack(jnp.split(near, rows, axis=1))
        return seq_sum(row_reduce(near))

    output_sum = spread_sum(d_attn, attended)
    heads_sum = spread_sum(act_in, d_qkv)

    parts = jnp.stack([jnp.sum(p, axis=0) for p in (input_part, mixer_part, before_part, after_part)])
    parts = jnp.transpose(parts.reshape(4, 4, dc), (1, 0, 2)).reshape(4, 4 * dc)
    extra = jnp.concatenate(
        [
            jnp.sum(query_part, axis=(0, 1)),
            jnp.sum(key_part, axis=0),
            jnp.stack(
                [jnp.sum(v * v * valid) for v in (block_out, branch_one, branch_two)]
            ),
        ]
    )
    cut = 8 * dc
    sent = jnp.concatenate([parts[2], parts[3], extra])
    kept = jnp.concatenate([parts[0], parts[1], extra]) + swap(sent, "col", 1)
    sent = jnp.concatenate([kept[cut // 2 : cut], kept[cut:]])
    kept = jnp.concatenate([kept[: cut // 2], kept[cut:]]) + swap(sent, "col", 2)
    for axis in ("seq", "row"):
        for step in bits_of(axis):
            kept = kept + swap(kept, axis, step)
    slope_gains = kept[: 4 * dc].reshape(4, dc) * inverse_root
    extra = kept[4 * dc :]
    slope_query, slope_key = extra[:HD] * inverse_root, extra[HD : 2 * HD] * inverse_root
    count = jnp.sum(valid_length).astype(f32) * D
    levels = jnp.sqrt(extra[2 * HD :] / count)

    m_shrink, nr_shrink, nl_shrink = shampoo(
        shrink_sum,
        inverse_root,
        jnp.transpose(shrink_weight),
        right_shrink[0, 0],
        left_shrink[0, 0],
        jnp.transpose(rightinv_shrink[0, 0]),
        jnp.transpose(leftinv_shrink[0, 0]),
    )
    expands = [
        shampoo(
            total,
            inverse_root,
            expand_weight[k],
            left_expand[k, 0, 0],
            right_expand[k, 0, 0],
            leftinv_expand[k, 0, 0],
            rightinv_expand[k, 0, 0],
        )
        for k, total in ((0, gate_sum), (1, upper_sum))
    ]
    m_output, nr_output, nl_output = shampoo(
        output_sum,
        inverse_root,
        jnp.transpose(output_weight),
        right_output[0, 0],
        left_output[0, 0],
        jnp.transpose(rightinv_output[0, 0]),
        jnp.transpose(leftinv_output[0, 0]),
    )
    m_heads, nl_heads, nr_heads = shampoo(
        heads_sum,
        inverse_root,
        heads_weight,
        left_heads[0, 0],
        right_heads[0, 0],
        leftinv_heads[0, 0],
        rightinv_heads[0, 0],
    )
    return (
        to_features(block_out)[None],
        to_features(input_slope)[None],
        slope_gains[0],
        slope_gains[1],
        slope_gains[2],
        slope_gains[3],
        slope_query,
        slope_key,
        heads_sum * inverse_root,
        m_heads,
        nl_heads[None, None],
        nr_heads[None, None],
        jnp.transpose(output_sum * inverse_root),
        jnp.transpose(m_output),
        nl_output[None, None],
        nr_output[None, None],
        jnp.stack([gate_sum, upper_sum]) * inverse_root,
        jnp.stack([e[0] for e in expands]),
        jnp.stack([e[1] for e in expands])[:, None, None],
        jnp.stack([e[2] for e in expands])[:, None, None],
        jnp.transpose(shrink_sum * inverse_root),
        jnp.transpose(m_shrink),
        nl_shrink[None, None],
        nr_shrink[None, None],
        levels[0],
        levels[1],
        levels[2],
    )


def solution(mesh):
    in_specs = (
        P("row", "seq", "col"),
        P("row", "seq", "col"),
        P("col", "row"),
        P("row", "col"),
        P(None, "col", "row"),
        P("row", "col"),
        P("col"),
        P("col"),
        P("col"),
        P("col"),
        P(),
        P(),
        P("col", None),
        P(),
        P("row", "col", None, None),
        P("row", "col", None, None),
        P("row", "col", None, None),
        P("row", "col", None, None),
        P("row", "col", None, None),
        P("row", "col", None, None),
        P("row", "col", None, None),
        P("row", "col", None, None),
        P(None, "row", "col", None, None),
        P(None, "row", "col", None, None),
        P(None, "row", "col", None, None),
        P(None, "row", "col", None, None),
        P("row", "col", None, None),
        P("row", "col", None, None),
        P("row", "col", None, None),
        P("row", "col", None, None),
    )
    out_specs = (
        P("row", "seq", "col"),
        P("row", "seq", "col"),
        P("col"),
        P("col"),
        P("col"),
        P("col"),
        P(),
        P(),
        P("col", "row"),
        P("col", "row"),
        P("row", "col", None, None),
        P("row", "col", None, None),
        P("row", "col"),
        P("row", "col"),
        P("row", "col", None, None),
        P("row", "col", None, None),
        P(None, "col", "row"),
        P(None, "col", "row"),
        P(None, "row", "col", None, None),
        P(None, "row", "col", None, None),
        P("row", "col"),
        P("row", "col"),
        P("row", "col", None, None),
        P("row", "col", None, None),
        P(),
        P(),
        P(),
    )
    return jax.shard_map(
        per_device, mesh=mesh, in_specs=in_specs, out_specs=out_specs, check_vma=False
    )
```
